256 devices in a mesh: seq: 32 (over z, y), head: 8 (over x, core).
Axes of the slice: x: 4, y: 4, z: 8, core: 2. Of those that a mesh axis runs over, the one named last changes fastest.
Arguments:
- queries: bfloat16 [16384, 32, 128], P('seq', 'head'), may hold values from -6 to 6
- key_matrix: bfloat16 [16384, 32, 128], P('seq', 'head'), may hold values from -6 to 6
- value_matrix: bfloat16 [16384, 32, 128], P('seq', 'head'), may hold values from -6 to 6
- level_weight: float32 [15, 32, 16384], P(None, 'head', 'seq'), may hold values from 0.25 to 4
- out_weight: bfloat16 [32, 128, 4096], P('head'), may hold values from -0.09375 to 0.09375
- grad_out: bfloat16 [16384, 4096], P('seq', 'head'), may hold values from -4 to 4
Outputs:
- mixed_out: bfloat16 [16384, 4096], P('seq', 'head')
- grad_queries: bfloat16 [16384, 32, 128], P('seq', 'head')
- grad_keys: bfloat16 [16384, 32, 128], P('seq', 'head')
- grad_values: bfloat16 [16384, 32, 128], P('seq', 'head')
- grad_levels: float32 [15, 32, 16384], P(None, 'head', 'seq')
The draws below stay inside these ranges and needn't reach their ends.
All inputs are finite; a program needn't handle non-finite values.
Results may differ from the reference program's by a relative error of at most 0.017.
Values may be sent and summed in bfloat16 or wider, within the bound.
No kernel may reach another device: no remote copies, remote signals or barrier semaphores. Data moves between devices by JAX's collectives and lax.ppermute only.
A program may use at most 128 MiB of HBM per device.

```python
import math
import jax
import jax.numpy as jnp
from jax import lax

D = 4096
HEADS = 32
HD = 128
TOK_DEV = 512
LOCAL = 9
CROSS = 5
LEVELS = 15
TOKENS = 16384
N_HEAD = 8


def shard_levels(rng, dims, pieces, smallest, high):
    factor_of = 1.0
    for dim, blocks in pieces:
        steps = jax.random.uniform(jax.random.fold_in(jax.random.fold_in(rng, 6), dim), (blocks,), jnp.float32, smallest / len(pieces), high / len(pieces))
        factor_of = factor_of * jnp.repeat(jnp.exp(steps), dims[dim] // blocks).reshape((-1,) + (1,) * (len(dims) - 1 - dim))
    return factor_of


def bell_draw(rng, extent, deviation, reach, split=(), kind=jnp.bfloat16):
    entries = jax.random.normal(rng, extent, jnp.float32) * deviation
    if len(split) > 0:
        entries = shard_levels(rng, extent, split, -0.22, 0.18) * entries
    return jnp.clip(entries, min=-reach, max=reach).astype(kind)


def setup_inputs(seed: int = 0) -> dict:
    seeds = jax.random.split(jax.random.key(seed), 7)
    queries = bell_draw(seeds[0], (TOKENS, HEADS, HD), 1.0, 6.0, ((0, 32), (1, 8)))
    key_matrix = bell_draw(seeds[1], (TOKENS, HEADS, HD), 1.0, 6.0, ((0, 32), (1, 8)))
    value_matrix = bell_draw(seeds[2], (TOKENS, HEADS, HD), 1.0, 6.0, ((0, 32), (1, 8)))
    level_weight = jnp.clip(jnp.exp(math.log(4.0) - 2.7725887 * jax.random.uniform(seeds[3], (LEVELS, HEADS, TOKENS), jnp.float32) ** shard_levels(seeds[3], (LEVELS, HEADS, TOKENS), ((1, 8), (2, 32)), -0.2, 0.2)), 0.25, 4.0)
    out_weight = bell_draw(seeds[4], (HEADS, HD, D), (HEADS * HD) ** -0.5, 0.09375, ((0, 8),))
    grad_out = bell_draw(seeds[5], (TOKENS, D), 0.5, 4.0, ((0, 32), (1, 8)))
    return {"queries": queries, "key_matrix": key_matrix, "value_matrix": value_matrix, "level_weight": level_weight, "out_weight": out_weight, "grad_out": grad_out}


PRECISE_MATCH = lax.Precision.HIGHEST

def top_bit(differ, bit_total):
    count_bits = jnp.zeros(differ.shape, jnp.int32)
    for exponent in range(bit_total):
        count_bits = count_bits + (differ >= 2 ** exponent).astype(jnp.int32)
    return count_bits

def level_scales(level_total, head_width):
    raised = jnp.maximum(jnp.arange(level_total, dtype=jnp.int32) - 1, 0).astype(jnp.float32)
    return jnp.exp2(-0.5 * raised) / jnp.sqrt(jnp.float32(head_width))

def block_sums(packed):
    query_part, key_portion, value_portion, mix_part, weight_part = packed
    key_weighted = jnp.einsum('gpl,gpq->plq', key_portion.astype(jnp.float32), value_portion.astype(jnp.float32), precision=PRECISE_MATCH)
    far_weights = weight_part[LOCAL + 1:]
    weighted = far_weights[:, :, :, None] * jnp.transpose(query_part.astype(jnp.float32), (1, 0, 2))[None]
    back_state = jnp.einsum('jhik,ihv->jhkv', weighted, mix_part.astype(jnp.float32), precision=PRECISE_MATCH)
    return (key_weighted, back_state)

def reference(queries, key_matrix, value_matrix, level_weight, out_weight, grad_out):
    blocks_total = TOKENS // TOK_DEV
    scales = level_scales(LEVELS, HD)
    weights_all = level_weight.astype(jnp.float32) * scales[:, None, None]
    flat_out = out_weight.reshape(HEADS * HD, D)
    grad_mix = lax.dot_general(grad_out, flat_out, (((1,), (1,)), ((), ())), preferred_element_type=jnp.float32)
    grad_mix = grad_mix.astype(jnp.bfloat16).reshape(blocks_total, TOK_DEV, HEADS, HD)
    queries_b = queries.reshape(blocks_total, TOK_DEV, HEADS, HD)
    keys_b = key_matrix.reshape(blocks_total, TOK_DEV, HEADS, HD)
    values_b = value_matrix.reshape(blocks_total, TOK_DEV, HEADS, HD)
    weights_b = jnp.transpose(weights_all.reshape(LEVELS, HEADS, blocks_total, TOK_DEV), (2, 0, 1, 3))
    key_states, query_states = lax.map(block_sums, (queries_b, keys_b, values_b, grad_mix, weights_b))
    later = lax.broadcasted_iota(jnp.int32, (blocks_total, blocks_total), 0)
    earlier = lax.broadcasted_iota(jnp.int32, (blocks_total, blocks_total), 1)
    block_gap = top_bit(jnp.bitwise_xor(later, earlier), CROSS)
    level_ladder = jnp.arange(1, CROSS + 1, dtype=jnp.int32)
    masks = ((block_gap[None] == level_ladder[:, None, None]) & (earlier < later)[None]).astype(jnp.float32)
    left_states = jnp.einsum('jde,ehkv->djhkv', masks, key_states, precision=PRECISE_MATCH)
    right_states = jnp.einsum('jde,djhkv->ejhkv', masks, query_states, precision=PRECISE_MATCH)

    def block_pass(packed):
        query_part, key_portion, value_portion, mix_part, weight_part, left_part, right_part = packed
        rows_index = lax.broadcasted_iota(jnp.int32, (TOK_DEV, TOK_DEV), 0)
        cols_index = lax.broadcasted_iota(jnp.int32, (TOK_DEV, TOK_DEV), 1)
        near_gap = top_bit(jnp.bitwise_xor(rows_index, cols_index), LOCAL)
        causal = cols_index <= rows_index
        query_f = query_part.astype(jnp.float32)
        key_f = key_portion.astype(jnp.float32)
        value_f = value_portion.astype(jnp.float32)
        mix_f = mix_part.astype(jnp.float32)
        scores = jnp.einsum('ihk,jhk->hij', query_f, key_f, precision=PRECISE_MATCH)
        mixing = jnp.zeros((HEADS, TOK_DEV, TOK_DEV), jnp.float32)
        for level_now in range(LOCAL + 1):
            chosen = ((near_gap == level_now) & causal)[None]
            mixing = jnp.where(chosen, weight_part[level_now][:, :, None], mixing)
        attention = lax.optimization_barrier((scores * mixing).astype(jnp.bfloat16)).astype(jnp.float32)
        local_out = jnp.einsum('hij,jhv->ihv', attention, value_f, precision=PRECISE_MATCH)
        far_rows = jnp.transpose(weight_part[LOCAL + 1:], (0, 2, 1))[..., None]
        reads = jnp.einsum('ihk,jhkv->jihv', query_f, left_part, precision=PRECISE_MATCH)
        attended = (local_out + lax.optimization_barrier(jnp.sum(far_rows * reads, axis=0))).astype(jnp.bfloat16)
        back = jnp.einsum('ihv,jhv->hij', mix_f, value_f, precision=PRECISE_MATCH)
        product = scores * back
        near_list = []
        for level_now in range(LOCAL + 1):
            chosen = ((near_gap == level_now) & causal)[None]
            near_list.append(lax.optimization_barrier(jnp.sum(jnp.where(chosen, product, 0.0), axis=2)))
        near_grad = jnp.stack(near_list) * scales[:LOCAL + 1, None, None]
        far_grad = jnp.transpose(lax.optimization_barrier(jnp.sum(reads * mix_f[None], axis=3)), (0, 2, 1)) * scales[LOCAL + 1:, None, None]
        grad_score = lax.optimization_barrier((back * mixing).astype(jnp.bfloat16)).astype(jnp.float32)
        grad_query = jnp.einsum('hij,jhk->ihk', grad_score, key_f, precision=PRECISE_MATCH)
        grad_query = grad_query + lax.optimization_barrier(jnp.sum(far_rows * jnp.einsum('jhkv,ihv->jihk', left_part, mix_f, precision=PRECISE_MATCH), axis=0))
        grad_key = jnp.einsum('hij,ihk->jhk', grad_score, query_f, precision=PRECISE_MATCH)
        grad_key = grad_key + jnp.einsum('jhkv,ihv->ihk', right_part, value_f, precision=PRECISE_MATCH)
        grad_value = jnp.einsum('hij,ihv->jhv', attention, mix_f, precision=PRECISE_MATCH)
        grad_value = grad_value + jnp.einsum('jhkv,ihk->ihv', right_part, key_f, precision=PRECISE_MATCH)
        return (attended, grad_query.astype(jnp.bfloat16), grad_key.astype(jnp.bfloat16), grad_value.astype(jnp.bfloat16), jnp.concatenate([near_grad, far_grad], 0))
    output_rows = lax.map(block_pass, (queries_b, keys_b, values_b, grad_mix, weights_b, left_states, right_states))
    attended = output_rows[0].reshape(TOKENS, HEADS * HD)
    group_width = HEADS * HD // N_HEAD
    summed = jnp.zeros((TOKENS, D), jnp.float32)
    for group in range(N_HEAD):
        lower_row = group * group_width
        partial_sum = jnp.dot(attended[:, lower_row:lower_row + group_width], flat_out[lower_row:lower_row + group_width], preferred_element_type=jnp.float32)
        summed = summed + lax.optimization_barrier(partial_sum.astype(jnp.bfloat16)).astype(jnp.float32)
    mixed_out = summed.astype(jnp.bfloat16)
    grad_queries = output_rows[1].reshape(TOKENS, HEADS, HD)
    grad_keys = output_rows[2].reshape(TOKENS, HEADS, HD)
    grad_values = output_rows[3].reshape(TOKENS, HEADS, HD)
    grad_levels = jnp.transpose(output_rows[4], (1, 2, 0, 3)).reshape(LEVELS, HEADS, TOKENS)
    return (mixed_out, grad_queries, grad_keys, grad_values, grad_levels)
```

```python
import math

import jax
import jax.numpy as jnp
from jax import lax
from jax.experimental import pallas as pl
from jax.experimental.pallas import tpu as pltpu
from jax.sharding import Mesh, PartitionSpec as P


F32 = jnp.float32
BF16 = jnp.bfloat16
BLK = 128
NEAR = 10
FAR = 5
HD = 128
C = [2.0 ** (-max(l - 1, 0) / 2) / math.sqrt(HD) for l in range(NEAR + FAR)]

NN = (((1,), (0,)), ((), ()))
NT = (((1,), (1,)), ((), ()))
TN = (((0,), (0,)), ((), ()))


def dot(a, b, dims):
    return lax.dot_general(a, b, dims, preferred_element_type=F32)


def diag_level():
    s = lax.broadcasted_iota(jnp.int32, (BLK, BLK), 0)
    t = lax.broadcasted_iota(jnp.int32, (BLK, BLK), 1)
    differ = s ^ t
    level = jnp.zeros((BLK, BLK), jnp.int32)
    for e in range(7):
        level = level + (differ >= 2**e).astype(jnp.int32)
    return jnp.where(s <= t, level, -1)


def w_row(lw_ref, l, h, i):
    return lw_ref[l, pl.ds(h, 1), pl.ds(i * BLK, BLK)] * C[l]


def mix_parts(lw_ref, level, h, i):
    diag = jnp.zeros((BLK, BLK), F32)
    for l in range(8):
        diag = jnp.where(level == l, w_row(lw_ref, l, h, i), diag)
    parts = []
    for j in range(i):
        parts.append(w_row(lw_ref, 8 if (i ^ j) == 1 else 9, h, i))
    return parts + [diag]


def flat(ref):
    rows, heads, hd = ref.shape
    return ref[...].reshape(rows, heads * hd)


def fwd_kernel(q_ref, k_ref, v_ref, lw_ref, lo_ref, wq_ref):
    level = diag_level()
    rows, heads, _ = q_ref.shape
    q_all, k_all, v_all = flat(q_ref), flat(k_ref), flat(v_ref)
    for h in range(heads):
        lanes = slice(h * HD, (h + 1) * HD)
        q, k, v = q_all[:, lanes], k_all[:, lanes], v_all[:, lanes]
        for i in range(rows // BLK):
            n = (i + 1) * BLK
            st = dot(k[:n], q[i * BLK : n], NT)
            mix = mix_parts(lw_ref, level, h, i)
            at = jnp.concatenate(
                [(st[j * BLK : (j + 1) * BLK] * mix[j]).astype(BF16) for j in range(i + 1)],
                axis=0,
            )
            lo_ref[pl.ds(i * BLK, BLK), lanes] = dot(at, v[:n], TN)
        qt = q.astype(F32).T
        for j in range(FAR):
            row = lw_ref[NEAR + j, pl.ds(h, 1), :] * C[NEAR + j]
            wq_ref[h, pl.ds(j * HD, HD), :] = (qt * row).astype(BF16)


def bwd_kernel(q_ref, k_ref, v_ref, g_ref, lw_ref, dq_ref, dk_ref, dv_ref, ng_ref):
    level = diag_level()
    rows, heads, _ = q_ref.shape
    blocks = rows // BLK
    q_all, k_all, v_all = flat(q_ref), flat(k_ref), flat(v_ref)
    for h in range(heads):
        lanes = slice(h * HD, (h + 1) * HD)
        q, k, v, g = q_all[:, lanes], k_all[:, lanes], v_all[:, lanes], g_ref[:, lanes]
        for i in reversed(range(blocks)):
            n = (i + 1) * BLK
            q_i, g_i = q[i * BLK : n], g[i * BLK : n]
            st = dot(k[:n], q_i, NT)
            bt = dot(v[:n], g_i, NT)
            mix = mix_parts(lw_ref, level, h, i)
            ats, gts, sums = [], [], [None] * NEAR
            for j in range(i + 1):
                s_j = st[j * BLK : (j + 1) * BLK]
                b_j = bt[j * BLK : (j + 1) * BLK]
                ats.append((s_j * mix[j]).astype(BF16))
                gts.append((b_j * mix[j]).astype(BF16))
                prod = s_j * b_j
                if j == i:
                    for l in range(8):
                        sums[l] = jnp.sum(
                            jnp.where(level == l, prod, 0.0), axis=0, keepdims=True
                        )
                else:
                    l = 8 if (i ^ j) == 1 else 9
                    total = jnp.sum(prod, axis=0, keepdims=True)
                    sums[l] = total if sums[l] is None else sums[l] + total
            at = jnp.concatenate(ats, axis=0)
            gt = jnp.concatenate(gts, axis=0)
            for l in range(NEAR):
                value = jnp.zeros((1, BLK), F32) if sums[l] is None else sums[l] * C[l]
                ng_ref[l, pl.ds(h, 1), pl.ds(i * BLK, BLK)] = value
            dq_ref[pl.ds(i * BLK, BLK), lanes] = dot(gt, k[:n], TN)
            if i == blocks - 1:
                dk_ref[:, lanes] = dot(gt, q_i, NN)
                dv_ref[:, lanes] = dot(at, g_i, NN)
            else:
                dk_ref[pl.ds(0, n), lanes] += dot(gt, q_i, NN)
                dv_ref[pl.ds(0, n), lanes] += dot(at, g_i, NN)


def left_stack(m_ref, r_refs, h):
    return jnp.concatenate(
        [(r[h].astype(F32) * m_ref[j]).astype(BF16) for j, r in enumerate(r_refs)], axis=0
    )


def attend_kernel(m_ref, lo_ref, wq_ref, r0, r1, r2, r3, r4, att_ref):
    for h in range(wq_ref.shape[0]):
        lanes = slice(h * HD, (h + 1) * HD)
        states = left_stack(m_ref, (r0, r1, r2, r3, r4), h)
        att_ref[:, lanes] = (lo_ref[:, lanes] + dot(wq_ref[h], states, TN)).astype(BF16)


def dq_kernel(m_ref, q_ref, g_ref, lw_ref, dql_ref, ng_ref, r0, r1, r2, r3, r4, dq_ref, gl_ref):
    _, heads, _ = q_ref.shape
    q_all = flat(q_ref)
    outs = []
    gl_ref[pl.ds(0, NEAR)] = ng_ref[...]
    for h in range(heads):
        lanes = slice(h * HD, (h + 1) * HD)
        states = left_stack(m_ref, (r0, r1, r2, r3, r4), h)
        read = dot(states, g_ref[:, lanes], NT)
        qt = q_all[:, lanes].astype(F32).T
        total = jnp.zeros(qt.shape, F32)
        for j in range(FAR):
            part = read[j * HD : (j + 1) * HD]
            row = lw_ref[NEAR + j, pl.ds(h, 1), :] * C[NEAR + j]
            total = total + part * row
            gl_ref[NEAR + j, pl.ds(h, 1), :] = (
                jnp.sum(part * qt, axis=0, keepdims=True) * C[NEAR + j]
            )
        outs.append((dql_ref[:, lanes] + total.T).astype(BF16))
    dq_ref[...] = jnp.concatenate(outs, axis=1).reshape(q_ref.shape)


def state_kernel(own_ref, rec_ref, wq_ref, g_ref, ws_ref):
    for h in range(wq_ref.shape[0]):
        lanes = slice(h * HD, (h + 1) * HD)
        g = (own_ref[:, lanes] + rec_ref[:, lanes].astype(F32)).astype(BF16)
        g_ref[:, lanes] = g
        ws_ref[h] = dot(wq_ref[h], g, NN).astype(BF16)


def final_kernel(dkl_ref, dvl_ref, k_ref, v_ref, r_ref, dk_ref, dv_ref):
    k_all, v_all = flat(k_ref), flat(v_ref)
    dks, dvs = [], []
    for h in range(r_ref.shape[0]):
        lanes = slice(h * HD, (h + 1) * HD)
        r = r_ref[h]
        dks.append((dkl_ref[:, lanes] + dot(v_all[:, lanes], r, NT)).astype(BF16))
        dvs.append((dvl_ref[:, lanes] + dot(k_all[:, lanes], r, NN)).astype(BF16))
    dk_ref[...] = jnp.concatenate(dks, axis=1).reshape(k_ref.shape)
    dv_ref[...] = jnp.concatenate(dvs, axis=1).reshape(k_ref.shape)


def wcol(ref, idx_ref, n, seg):
    return ref[:, pl.ds(pl.multiple_of(idx_ref[n] * seg, seg), seg)]


def mix12_kernel(idx_ref, go, gl, gr, w_ref, p_ref, own_ref, par_ref):
    seg = go.shape[1]
    for ref, out in ((p_ref, par_ref), (w_ref, own_ref)):
        out[...] = (
            dot(go[...], wcol(ref, idx_ref, 0, seg), NT)
            + dot(gl[...], wcol(ref, idx_ref, 1, seg), NT)
            + dot(gr[...], wcol(ref, idx_ref, 2, seg), NT)
        )


def mix3_kernel(idx_ref, top, bot, acc, w_ref, out_ref):
    half, seg = top.shape
    w = wcol(w_ref, idx_ref, 3, seg)
    for base, part in ((0, top), (half, bot)):
        rows = pl.ds(base, half)
        out_ref[rows, :] = (acc[rows, :] + dot(part[...], w, NT)).astype(out_ref.dtype)


def out_rows(idx_ref, a, ap, w_ref, p_ref, n, rows, seg):
    return dot(a[rows, :], wcol(w_ref, idx_ref, n, seg), NN) + dot(
        ap[rows, :], wcol(p_ref, idx_ref, n, seg), NN
    )


def out_far_kernel(idx_ref, a, ap, w_ref, p_ref, top_ref, bot_ref):
    half, seg = top_ref.shape
    for ref, base in ((top_ref, 0), (bot_ref, half)):
        ref[...] = out_rows(idx_ref, a, ap, w_ref, p_ref, 3, pl.ds(base, half), seg).astype(BF16)


def out_first_kernel(idx_ref, a, ap, w_ref, p_ref, r_bot, l_top):
    half, seg = r_bot.shape
    r_bot[...] = out_rows(idx_ref, a, ap, w_ref, p_ref, 2, pl.ds(half, half), seg).astype(BF16)
    l_top[...] = out_rows(idx_ref, a, ap, w_ref, p_ref, 1, pl.ds(0, half), seg).astype(BF16)


def out_rest_kernel(idx_ref, a, ap, w_ref, p_ref, r_top, l_bot, own):
    half, seg = r_top.shape
    r_top[...] = out_rows(idx_ref, a, ap, w_ref, p_ref, 2, pl.ds(0, half), seg)
    l_bot[...] = out_rows(idx_ref, a, ap, w_ref, p_ref, 1, pl.ds(half, half), seg)
    own[...] = out_rows(idx_ref, a, ap, w_ref, p_ref, 0, pl.ds(0, 2 * half), seg)


def sum_kernel(own, lt, lb, rt, rb, out_ref):
    half = lt.shape[0]
    for base, a, b in ((0, lt, rt), (half, lb, rb)):
        rows = pl.ds(base, half)
        out_ref[rows, :] = (own[rows, :] + a[...].astype(F32) + b[...].astype(F32)).astype(BF16)


SMEM = pl.BlockSpec(memory_space=pltpu.SMEM)
VMEM = pl.BlockSpec(memory_space=pltpu.VMEM)


def kernel_call(body, outs, operands, flops, scalars=0, vmem=16):
    out_shape = [jax.ShapeDtypeStruct(s, d) for s, d in outs]
    nbytes = sum(math.prod(s) * jnp.dtype(d).itemsize for s, d in outs)
    nbytes += sum(o.size * o.dtype.itemsize for o in operands)
    return pl.pallas_call(
        body,
        in_specs=[SMEM] * scalars + [VMEM] * (len(operands) - scalars),
        out_specs=[VMEM] * len(outs),
        out_shape=out_shape,
        cost_estimate=pl.CostEstimate(
            flops=int(flops), transcendentals=0, bytes_accessed=int(nbytes)
        ),
        compiler_params=pltpu.CompilerParams(vmem_limit_bytes=vmem << 20),
    )(*operands)


def body(queries, key_matrix, value_matrix, level_weight, out_weight, grad_out):
    rows, heads, hd = queries.shape
    width = heads * hd
    feat = out_weight.shape[2]
    levels = level_weight.shape[0]
    half = rows // 2
    z, y, x, c = (lax.axis_index(n) for n in ("z", "y", "x", "c"))
    nx, ny, nz = (lax.axis_size(n) for n in ("x", "y", "z"))
    right = [(i, (i + 1) % nx) for i in range(nx)]
    left = [(i, (i - 1) % nx) for i in range(nx)]
    swap = [(0, 1), (1, 0)]
    seg = feat // (2 * nx)
    w2 = out_weight.reshape(width, feat)

    from_l = lax.ppermute(grad_out, "x", right)
    from_r = lax.ppermute(grad_out, "x", left)
    w_par = lax.ppermute(w2, "c", swap)

    run = jnp.einsum("gpl,gpq->plq", key_matrix, value_matrix, preferred_element_type=F32)
    lefts = []
    for step, (axis, bit) in enumerate((("y", 0), ("y", 1), ("z", 0), ("z", 1), ("z", 2))):
        n = lax.axis_size(axis)
        last = step == 4
        route = [(i, i ^ (1 << bit)) for i in range(n) if not (last and i >> bit & 1)]
        got = lax.ppermute(run.astype(BF16), axis, route)
        lefts.append(got)
        if not last:
            run = run + got.astype(F32)
    bits = [y & 1, y >> 1 & 1, z & 1, z >> 1 & 1, z >> 2 & 1]
    mask = jnp.stack(bits).astype(F32)

    block = 2 * rows * rows * width
    local_out, wq = kernel_call(
        fwd_kernel,
        [((rows, width), F32), ((heads, FAR * hd, rows), BF16)],
        (queries, key_matrix, value_matrix, level_weight),
        2 * block,
    )

    xs = jnp.stack([x, (x + nx - 1) % nx, (x + 1) % nx, (x + 2) % nx])
    idx = (xs * 2 + c).astype(jnp.int32)

    far_top = lax.ppermute(from_l[:half], "x", right)
    far_bot = lax.ppermute(from_r[half:], "x", left)
    mm = 2 * rows * seg * width
    own12, par12 = kernel_call(
        mix12_kernel,
        [((rows, width), F32)] * 2,
        (idx, grad_out, from_l, from_r, w2, w_par),
        6 * mm,
        scalars=1,
    )
    (mix_send,) = kernel_call(
        mix3_kernel, [((rows, width), BF16)], (idx, far_top, far_bot, par12, w_par), mm, scalars=1
    )
    mix_got = lax.ppermute(mix_send, "c", swap)
    (mix_own,) = kernel_call(
        mix3_kernel, [((rows, width), F32)], (idx, far_top, far_bot, own12, w2), mm, scalars=1
    )
    g2, ws = kernel_call(
        state_kernel,
        [((rows, width), BF16), ((heads, FAR * hd, hd), BF16)],
        (mix_own, mix_got, wq),
        2 * rows * hd * hd * FAR * heads,
    )

    got = lax.all_to_all(ws, "y", split_axis=0, concat_axis=0, tiled=True)
    got = got.reshape(ny, FAR, hd, hd).astype(F32)
    pairs = got[2, 1] + got[3, 1]
    near = [got[1, 0] + pairs, pairs, got[3, 0], jnp.zeros_like(pairs)]
    held = got[:, 2:].sum(axis=0)
    acc = jnp.zeros_like(pairs)
    for bit in range(3):
        route = [(i, i ^ (1 << bit)) for i in range(nz)]
        other = lax.ppermute(held.astype(BF16), "z", route).astype(F32)
        acc = acc + jnp.where(z >> bit & 1, 0.0, other[0])
        held = held[1:] + other[1:]
    back = jnp.stack([part + acc for part in near]).astype(BF16)
    right_states = lax.all_to_all(back, "y", split_axis=0, concat_axis=0, tiled=True)

    (attended,) = kernel_call(
        attend_kernel,
        [((rows, width), BF16)],
        (mask, local_out, wq, *lefts),
        2 * rows * hd * hd * FAR * heads,
        scalars=1,
    )
    att_par = lax.ppermute(attended, "c", swap)

    piece = ((half, seg), BF16)
    piece32 = ((half, seg), F32)
    operands = (idx, attended, att_par, w2, w_par)
    opp_top, opp_bot = kernel_call(out_far_kernel, [piece] * 2, operands, 2 * mm, scalars=1)
    via_l = lax.ppermute(opp_top, "x", right)
    via_r = lax.ppermute(opp_bot, "x", left)
    r_bot, l_top = kernel_call(out_first_kernel, [piece] * 2, operands, 2 * mm, scalars=1)
    in_l_bot = lax.ppermute(r_bot, "x", right)
    in_r_top = lax.ppermute(l_top, "x", left)
    r_top, l_bot, out_own = kernel_call(
        out_rest_kernel, [piece32, piece32, ((rows, seg), F32)], operands, 4 * mm, scalars=1
    )
    r_top = (r_top + via_l.astype(F32)).astype(BF16)
    l_bot = (l_bot + via_r.astype(F32)).astype(BF16)
    in_l_top = lax.ppermute(r_top, "x", right)
    in_r_bot = lax.ppermute(l_bot, "x", left)
    (mixed_out,) = kernel_call(
        sum_kernel,
        [((rows, seg), BF16)],
        (out_own, in_l_top, in_l_bot, in_r_top, in_r_bot),
        rows * seg * 4,
    )

    dq_local, dk_local, dv_local, near_grad = kernel_call(
        bwd_kernel,
        [((rows, width), F32)] * 3 + [((NEAR, heads, rows), F32)],
        (queries, key_matrix, value_matrix, g2, level_weight),
        5 * block,
    )
    grad_queries, grad_levels = kernel_call(
        dq_kernel,
        [((rows, heads, hd), BF16), ((levels, heads, rows), F32)],
        (mask, queries, g2, level_weight, dq_local, near_grad, *lefts),
        2 * rows * hd * hd * FAR * heads,
        scalars=1,
    )
    grad_keys, grad_values = kernel_call(
        final_kernel,
        [((rows, heads, hd), BF16)] * 2,
        (dk_local, dv_local, key_matrix, value_matrix, right_states),
        4 * rows * hd * hd * heads,
    )
    return mixed_out, grad_queries, grad_keys, grad_values, grad_levels


def solution(mesh):
    grid = Mesh(mesh.devices.reshape(8, 4, 4, 2), ("z", "y", "x", "c"))
    seq, head = ("z", "y"), ("x", "c")
    by_row = P(seq, head, None)
    in_specs = (by_row, by_row, by_row, P(None, head, seq), P(head, None, None), P(seq, head))
    out_specs = (P(seq, head), by_row, by_row, by_row, P(None, head, seq))
    return jax.shard_map(body, mesh=grid, in_specs=in_specs, out_specs=out_specs, check_vma=False)
```

```python
import math

import jax
import jax.numpy as jnp
from jax import lax
from jax.experimental import pallas as pl
from jax.experimental.pallas import tpu as pltpu
from jax.sharding import Mesh, PartitionSpec as P


F32 = jnp.float32
BF16 = jnp.bfloat16
BLK = 128
NEAR = 10
FAR = 5
NX = 4
HD = 128
C = [2.0 ** (-max(l - 1, 0) / 2) / math.sqrt(HD) for l in range(NEAR + FAR)]

NN = (((1,), (0,)), ((), ()))
NT = (((1,), (1,)), ((), ()))
TN = (((0,), (0,)), ((), ()))


def dot(a, b, dims):
    return lax.dot_general(a, b, dims, preferred_element_type=F32)


def diag_level():
    s = lax.broadcasted_iota(jnp.int32, (BLK, BLK), 0)
    t = lax.broadcasted_iota(jnp.int32, (BLK, BLK), 1)
    differ = s ^ t
    level = jnp.zeros((BLK, BLK), jnp.int32)
    for e in range(7):
        level = level + (differ >= 2**e).astype(jnp.int32)
    return jnp.where(s <= t, level, -1)


def w_row(lw_ref, l, h, i):
    return lw_ref[l, pl.ds(h, 1), pl.ds(i * BLK, BLK)] * C[l]


def mix_parts(lw_ref, level, h, i):
    diag = jnp.zeros((BLK, BLK), F32)
    for l in range(8):
        diag = jnp.where(level == l, w_row(lw_ref, l, h, i), diag)
    parts = []
    for j in range(i):
        parts.append(w_row(lw_ref, 8 if (i ^ j) == 1 else 9, h, i))
    return parts + [diag]


def flat(ref):
    rows, heads, hd = ref.shape
    return ref[...].reshape(rows, heads * hd)


def fwd_kernel(q_ref, k_ref, v_ref, lw_ref, lo_ref, wq_ref):
    level = diag_level()
    rows, heads, _ = q_ref.shape
    q_all, k_all, v_all = flat(q_ref), flat(k_ref), flat(v_ref)
    for h in range(heads):
        lanes = slice(h * HD, (h + 1) * HD)
        q, k, v = q_all[:, lanes], k_all[:, lanes], v_all[:, lanes]
        for i in range(rows // BLK):
            n = (i + 1) * BLK
            st = dot(k[:n], q[i * BLK : n], NT)
            mix = mix_parts(lw_ref, level, h, i)
            at = jnp.concatenate(
                [(st[j * BLK : (j + 1) * BLK] * mix[j]).astype(BF16) for j in range(i + 1)],
                axis=0,
            )
            lo_ref[pl.ds(i * BLK, BLK), lanes] = dot(at, v[:n], TN)
        qt = q.astype(F32).T
        for j in range(FAR):
            row = lw_ref[NEAR + j, pl.ds(h, 1), :] * C[NEAR + j]
            wq_ref[h, pl.ds(j * HD, HD), :] = (qt * row).astype(BF16)


def bwd_kernel(q_ref, k_ref, v_ref, g_ref, lw_ref, dq_ref, dk_ref, dv_ref, ng_ref):
    level = diag_level()
    rows, heads, _ = q_ref.shape
    blocks = rows // BLK
    q_all, k_all, v_all = flat(q_ref), flat(k_ref), flat(v_ref)
    for h in range(heads):
        lanes = slice(h * HD, (h + 1) * HD)
        q, k, v, g = q_all[:, lanes], k_all[:, lanes], v_all[:, lanes], g_ref[:, lanes]
        for i in reversed(range(blocks)):
            n = (i + 1) * BLK
            q_i, g_i = q[i * BLK : n], g[i * BLK : n]
            st = dot(k[:n], q_i, NT)
            bt = dot(v[:n], g_i, NT)
            mix = mix_parts(lw_ref, level, h, i)
            ats, gts, sums = [], [], [None] * NEAR
            for j in range(i + 1):
                s_j = st[j * BLK : (j + 1) * BLK]
                b_j = bt[j * BLK : (j + 1) * BLK]
                ats.append((s_j * mix[j]).astype(BF16))
                gts.append((b_j * mix[j]).astype(BF16))
                prod = s_j * b_j
                if j == i:
                    for l in range(8):
                        sums[l] = jnp.sum(
                            jnp.where(level == l, prod, 0.0), axis=0, keepdims=True
                        )
                else:
                    l = 8 if (i ^ j) == 1 else 9
                    total = jnp.sum(prod, axis=0, keepdims=True)
                    sums[l] = total if sums[l] is None else sums[l] + total
            at = jnp.concatenate(ats, axis=0)
            gt = jnp.concatenate(gts, axis=0)
            for l in range(NEAR):
                value = jnp.zeros((1, BLK), F32) if sums[l] is None else sums[l] * C[l]
                ng_ref[l, pl.ds(h, 1), pl.ds(i * BLK, BLK)] = value
            dq_ref[pl.ds(i * BLK, BLK), lanes] = dot(gt, k[:n], TN)
            if i == blocks - 1:
                dk_ref[:, lanes] = dot(gt, q_i, NN)
                dv_ref[:, lanes] = dot(at, g_i, NN)
            else:
                dk_ref[pl.ds(0, n), lanes] += dot(gt, q_i, NN)
                dv_ref[pl.ds(0, n), lanes] += dot(at, g_i, NN)


def bit_of(axis, bit):
    return lax.rem(lax.div(lax.axis_index(axis), 1 << bit), 2)


def tree_bits():
    return [bit_of("y", 0), bit_of("y", 1), bit_of("z", 0), bit_of("z", 1), bit_of("z", 2)]


def left_stack(r_refs, h):
    return jnp.concatenate(
        [
            (r[h].astype(F32) * b.astype(F32)).astype(BF16)
            for b, r in zip(tree_bits(), r_refs, strict=True)
        ],
        axis=0,
    )


def attend_kernel(lo_ref, wq_ref, r0, r1, r2, r3, r4, att_ref):
    for h in range(wq_ref.shape[0]):
        lanes = slice(h * HD, (h + 1) * HD)
        states = left_stack((r0, r1, r2, r3, r4), h)
        att_ref[:, lanes] = (lo_ref[:, lanes] + dot(wq_ref[h], states, TN)).astype(BF16)


def dq_kernel(q_ref, g_ref, lw_ref, dql_ref, ng_ref, r0, r1, r2, r3, r4, dq_ref, gl_ref):
    _, heads, _ = q_ref.shape
    q_all = flat(q_ref)
    outs = []
    gl_ref[pl.ds(0, NEAR)] = ng_ref[...]
    for h in range(heads):
        lanes = slice(h * HD, (h + 1) * HD)
        states = left_stack((r0, r1, r2, r3, r4), h)
        read = dot(states, g_ref[:, lanes], NT)
        qt = q_all[:, lanes].astype(F32).T
        total = jnp.zeros(qt.shape, F32)
        for j in range(FAR):
            part = read[j * HD : (j + 1) * HD]
            row = lw_ref[NEAR + j, pl.ds(h, 1), :] * C[NEAR + j]
            total = total + part * row
            gl_ref[NEAR + j, pl.ds(h, 1), :] = (
                jnp.sum(part * qt, axis=0, keepdims=True) * C[NEAR + j]
            )
        outs.append((dql_ref[:, lanes] + total.T).astype(BF16))
    dq_ref[...] = jnp.concatenate(outs, axis=1).reshape(q_ref.shape)


def swapped(m):
    b0, b1 = bit_of("y", 0), bit_of("y", 1)
    low = 1 - b0 if m & 1 else b0
    high = 1 - b1 if m & 2 else b1
    return high * 2 + low


def state_kernel(own_ref, rec_ref, wq_ref, g_ref, *ws_refs):
    g_ref[...] = (own_ref[...] + rec_ref[...].astype(F32)).astype(BF16)
    for m, ws_ref in enumerate(ws_refs):
        h = swapped(m)
        g = g_ref[:, pl.ds(pl.multiple_of(h * HD, HD), HD)]
        ws_ref[...] = dot(wq_ref[h], g, NN).astype(BF16).reshape(FAR, HD, HD)


def rsum_kernel(w0, w1, w2, w3, near_ref, held_ref, send_ref):
    w = (w0, w1, w2, w3)
    b0, b1 = bit_of("y", 0), bit_of("y", 1)
    low = [(1 - b0 if n & 1 else b0).astype(F32) for n in range(4)]
    high = [(1 - b1 if n & 2 else b1).astype(F32) for n in range(4)]
    first = [w[n][0].astype(F32) * low[n] for n in range(4)]
    second = [w[n][1].astype(F32) * high[n] for n in range(4)]
    for m in range(4):
        near_ref[m] = first[m ^ 1] + second[m ^ 2] + second[m ^ 3]
    for j in range(2, FAR):
        total = sum(w[n][j].astype(F32) for n in range(4))
        held_ref[j - 2] = total
        send_ref[j - 2] = total.astype(BF16)


def tree0_kernel(held_ref, got_ref, acc_ref, next_ref, send_ref):
    off = (1 - bit_of("z", 0)).astype(F32)
    acc_ref[...] = got_ref[0].astype(F32) * off
    for j in range(2):
        total = held_ref[j + 1] + got_ref[j + 1].astype(F32)
        next_ref[j] = total
        send_ref[j] = total.astype(BF16)


def tree1_kernel(acc_in, held_ref, got_ref, acc_ref, send_ref):
    off = (1 - bit_of("z", 1)).astype(F32)
    acc_ref[...] = acc_in[...] + got_ref[0].astype(F32) * off
    send_ref[0] = (held_ref[1] + got_ref[1].astype(F32)).astype(BF16)


def tree2_kernel(acc_in, near_ref, got_ref, *out_refs):
    off = (1 - bit_of("z", 2)).astype(F32)
    acc = acc_in[...] + got_ref[0].astype(F32) * off
    for m, ref in enumerate(out_refs):
        ref[...] = (near_ref[m] + acc).astype(BF16)


def final_kernel(dkl_ref, dvl_ref, k_ref, v_ref, r0, r1, r2, r3, dk_ref, dv_ref, r_ref):
    k_all, v_all = flat(k_ref), flat(v_ref)
    for m, r in enumerate((r0, r1, r2, r3)):
        r_ref[swapped(m)] = r[...]
    dks, dvs = [], []
    for h in range(r_ref.shape[0]):
        lanes = slice(h * HD, (h + 1) * HD)
        r = r_ref[h]
        dks.append((dkl_ref[:, lanes] + dot(v_all[:, lanes], r, NT)).astype(BF16))
        dvs.append((dvl_ref[:, lanes] + dot(k_all[:, lanes], r, NN)).astype(BF16))
    dk_ref[...] = jnp.concatenate(dks, axis=1).reshape(k_ref.shape)
    dv_ref[...] = jnp.concatenate(dvs, axis=1).reshape(k_ref.shape)


def wcol(ref, n, seg):
    steps = (0, NX - 1, 1, 2)[n]
    at = lax.rem(lax.axis_index("x") + steps, NX) * 2 + lax.axis_index("c")
    return ref[:, pl.ds(pl.multiple_of(at * seg, seg), seg)]


def mix12_kernel(go, gl, gr, w_ref, p_ref, own_ref, par_ref):
    seg = go.shape[1]
    for ref, out in ((p_ref, par_ref), (w_ref, own_ref)):
        out[...] = (
            dot(go[...], wcol(ref, 0, seg), NT)
            + dot(gl[...], wcol(ref, 1, seg), NT)
            + dot(gr[...], wcol(ref, 2, seg), NT)
        )


def mix3_kernel(top, bot, acc, w_ref, out_ref):
    half, seg = top.shape
    w = wcol(w_ref, 3, seg)
    for base, part in ((0, top), (half, bot)):
        rows = pl.ds(base, half)
        out_ref[rows, :] = (acc[rows, :] + dot(part[...], w, NT)).astype(out_ref.dtype)


def out_rows(a, ap, w_ref, p_ref, n, rows, seg):
    return dot(a[rows, :], wcol(w_ref, n, seg), NN) + dot(
        ap[rows, :], wcol(p_ref, n, seg), NN
    )


def out_far_kernel(a, ap, w_ref, p_ref, top_ref, bot_ref):
    half, seg = top_ref.shape
    for ref, base in ((top_ref, 0), (bot_ref, half)):
        ref[...] = out_rows(a, ap, w_ref, p_ref, 3, pl.ds(base, half), seg).astype(BF16)


def out_rest_kernel(a, ap, w_ref, p_ref, r_bot, l_top, r_top, l_bot, own):
    half, seg = r_bot.shape
    top, bot = pl.ds(0, half), pl.ds(half, half)
    r_bot[...] = out_rows(a, ap, w_ref, p_ref, 2, bot, seg).astype(BF16)
    l_top[...] = out_rows(a, ap, w_ref, p_ref, 1, top, seg).astype(BF16)
    r_top[...] = out_rows(a, ap, w_ref, p_ref, 2, top, seg)
    l_bot[...] = out_rows(a, ap, w_ref, p_ref, 1, bot, seg)
    own[...] = out_rows(a, ap, w_ref, p_ref, 0, pl.ds(0, 2 * half), seg)


def join_kernel(r_top, l_bot, via_l, via_r, r_out, l_out):
    r_out[...] = (r_top[...] + via_l[...].astype(F32)).astype(BF16)
    l_out[...] = (l_bot[...] + via_r[...].astype(F32)).astype(BF16)


def sum_kernel(own, l_top, l_bot, r_top, r_bot, out_ref):
    half = l_top.shape[0]
    for base, a, b in ((0, l_top, r_top), (half, l_bot, r_bot)):
        rows = pl.ds(base, half)
        out_ref[rows, :] = (own[rows, :] + a[...].astype(F32) + b[...].astype(F32)).astype(BF16)


VMEM = pl.BlockSpec(memory_space=pltpu.VMEM)


def kernel_call(body, outs, operands, flops, scratch=(), vmem=16):
    out_shape = [jax.ShapeDtypeStruct(s, d) for s, d in outs]
    nbytes = sum(math.prod(s) * jnp.dtype(d).itemsize for s, d in outs)
    nbytes += sum(o.size * o.dtype.itemsize for o in operands)
    return pl.pallas_call(
        body,
        in_specs=[VMEM] * len(operands),
        out_specs=[VMEM] * len(outs),
        out_shape=out_shape,
        scratch_shapes=list(scratch),
        cost_estimate=pl.CostEstimate(
            flops=int(flops), transcendentals=0, bytes_accessed=int(nbytes)
        ),
        compiler_params=pltpu.CompilerParams(vmem_limit_bytes=vmem << 20),
    )(*operands)


def body(queries, key_matrix, value_matrix, level_weight, out_weight, grad_out):
    rows, heads, hd = queries.shape
    width = heads * hd
    feat = out_weight.shape[2]
    levels = level_weight.shape[0]
    half = rows // 2
    nx, ny, nz = (lax.axis_size(n) for n in ("x", "y", "z"))
    right = [(i, (i + 1) % nx) for i in range(nx)]
    left = [(i, (i - 1) % nx) for i in range(nx)]
    swap = [(0, 1), (1, 0)]
    seg = feat // (2 * nx)
    w2 = out_weight.reshape(width, feat)

    from_l = lax.ppermute(grad_out, "x", right)
    from_r = lax.ppermute(grad_out, "x", left)
    w_par = lax.ppermute(w2, "c", swap)

    run = jnp.einsum("gpl,gpq->plq", key_matrix, value_matrix, preferred_element_type=F32)
    lefts = []
    for step, (axis, bit) in enumerate((("y", 0), ("y", 1), ("z", 0), ("z", 1), ("z", 2))):
        n = lax.axis_size(axis)
        last = step == 4
        route = [(i, i ^ (1 << bit)) for i in range(n) if not (last and i >> bit & 1)]
        got = lax.ppermute(run.astype(BF16), axis, route)
        lefts.append(got)
        if not last:
            run = run + got.astype(F32)
    block = 2 * rows * rows * width
    local_out, wq = kernel_call(
        fwd_kernel,
        [((rows, width), F32), ((heads, FAR * hd, rows), BF16)],
        (queries, key_matrix, value_matrix, level_weight),
        2 * block,
    )

    far_top = lax.ppermute(from_l[:half], "x", right)
    far_bot = lax.ppermute(from_r[half:], "x", left)
    mm = 2 * rows * seg * width
    own12, par12 = kernel_call(
        mix12_kernel, [((rows, width), F32)] * 2, (grad_out, from_l, from_r, w2, w_par), 6 * mm
    )
    (mix_send,) = kernel_call(
        mix3_kernel, [((rows, width), BF16)], (far_top, far_bot, par12, w_par), mm
    )
    mix_got = lax.ppermute(mix_send, "c", swap)
    (mix_own,) = kernel_call(mix3_kernel, [((rows, width), F32)], (far_top, far_bot, own12, w2), mm)
    square = (hd, hd)
    g2, *ws = kernel_call(
        state_kernel,
        [((rows, width), BF16)] + [((FAR, *square), BF16)] * ny,
        (mix_own, mix_got, wq),
        2 * rows * hd * hd * FAR * heads,
    )

    def across_y(parts):
        arrived = [parts[0]]
        for m in range(1, ny):
            arrived.append(lax.ppermute(parts[m], "y", [(i, i ^ m) for i in range(ny)]))
        return arrived

    def across_z(bit, value):
        return lax.ppermute(value, "z", [(i, i ^ (1 << bit)) for i in range(nz)])

    tiny = 8 * hd * hd
    near, held, send = kernel_call(
        rsum_kernel,
        [((ny, *square), F32), ((3, *square), F32), ((3, *square), BF16)],
        across_y(ws),
        tiny,
    )
    acc, held, send = kernel_call(
        tree0_kernel,
        [(square, F32), ((2, *square), F32), ((2, *square), BF16)],
        (held, across_z(0, send)),
        tiny,
    )
    acc, send = kernel_call(
        tree1_kernel, [(square, F32), ((1, *square), BF16)], (acc, held, across_z(1, send)), tiny
    )
    back = kernel_call(tree2_kernel, [(square, BF16)] * ny, (acc, near, across_z(2, send)), tiny)
    right_states = across_y(back)

    (attended,) = kernel_call(
        attend_kernel,
        [((rows, width), BF16)],
        (local_out, wq, *lefts),
        2 * rows * hd * hd * FAR * heads,
    )
    att_par = lax.ppermute(attended, "c", swap)

    piece = ((half, seg), BF16)
    piece32 = ((half, seg), F32)
    operands = (attended, att_par, w2, w_par)
    opp_top, opp_bot = kernel_call(out_far_kernel, [piece] * 2, operands, 2 * mm)
    via_l = lax.ppermute(opp_top, "x", right)
    via_r = lax.ppermute(opp_bot, "x", left)
    r_bot, l_top, r_top, l_bot, out_own = kernel_call(
        out_rest_kernel, [piece] * 2 + [piece32] * 2 + [((rows, seg), F32)], operands, 6 * mm
    )
    in_l_bot = lax.ppermute(r_bot, "x", right)
    in_r_top = lax.ppermute(l_top, "x", left)
    r_top, l_bot = kernel_call(
        join_kernel, [piece] * 2, (r_top, l_bot, via_l, via_r), rows * seg * 2
    )
    in_l_top = lax.ppermute(r_top, "x", right)
    in_r_bot = lax.ppermute(l_bot, "x", left)
    (mixed_out,) = kernel_call(
        sum_kernel,
        [((rows, seg), BF16)],
        (out_own, in_l_top, in_l_bot, in_r_top, in_r_bot),
        rows * seg * 4,
    )

    dq_local, dk_local, dv_local, near_grad = kernel_call(
        bwd_kernel,
        [((rows, width), F32)] * 3 + [((NEAR, heads, rows), F32)],
        (queries, key_matrix, value_matrix, g2, level_weight),
        5 * block,
    )
    grad_queries, grad_levels = kernel_call(
        dq_kernel,
        [((rows, heads, hd), BF16), ((levels, heads, rows), F32)],
        (queries, g2, level_weight, dq_local, near_grad, *lefts),
        2 * rows * hd * hd * FAR * heads,
    )
    grad_keys, grad_values = kernel_call(
        final_kernel,
        [((rows, heads, hd), BF16)] * 2,
        (dk_local, dv_local, key_matrix, value_matrix, *right_states),
        4 * rows * hd * hd * heads,
        scratch=[pltpu.VMEM((heads, hd, hd), BF16)],
    )
    return mixed_out, grad_queries, grad_keys, grad_values, grad_levels


def solution(mesh):
    grid = Mesh(mesh.devices.reshape(8, 4, 4, 2), ("z", "y", "x", "c"))
    seq, head = ("z", "y"), ("x", "c")
    by_row = P(seq, head, None)
    in_specs = (by_row, by_row, by_row, P(None, head, seq), P(head, None, None), P(seq, head))
    out_specs = (P(seq, head), by_row, by_row, by_row, P(None, head, seq))
    return jax.shard_map(body, mesh=grid, in_specs=in_specs, out_specs=out_specs, check_vma=False)
```

```python
import functools
import math

import jax
import jax.numpy as jnp
from jax import lax
from jax.experimental import pallas as pl
from jax.experimental.pallas import tpu as pltpu
from jax.sharding import Mesh, PartitionSpec as P


F32 = jnp.float32
BF16 = jnp.bfloat16
BLK = 128
NEAR = 10
FAR = 5
NX = 4
HD = 128
C = [2.0 ** (-max(l - 1, 0) / 2) / math.sqrt(HD) for l in range(NEAR + FAR)]

NN = (((1,), (0,)), ((), ()))
NT = (((1,), (1,)), ((), ()))
TN = (((0,), (0,)), ((), ()))


def dot(a, b, dims):
    return lax.dot_general(a, b, dims, preferred_element_type=F32)


def diag_level():
    s = lax.broadcasted_iota(jnp.int32, (BLK, BLK), 0)
    t = lax.broadcasted_iota(jnp.int32, (BLK, BLK), 1)
    differ = s ^ t
    level = jnp.zeros((BLK, BLK), jnp.int32)
    for e in range(7):
        level = level + (differ >= 2**e).astype(jnp.int32)
    return jnp.where(s <= t, level, -1)


def w_row(lw_ref, l, h, i):
    return lw_ref[l, pl.ds(h, 1), pl.ds(i * BLK, BLK)] * C[l]


def mix_parts(lw_ref, level, h, i):
    diag = jnp.zeros((BLK, BLK), F32)
    for l in range(8):
        diag = jnp.where(level == l, w_row(lw_ref, l, h, i), diag)
    parts = []
    for j in range(i):
        parts.append(w_row(lw_ref, 8 if (i ^ j) == 1 else 9, h, i))
    return parts + [diag]


def flat(ref):
    rows, heads, hd = ref.shape
    return ref[...].reshape(rows, heads * hd)


def stage_kernel(*refs):
    n = (len(refs) - 1) // 2
    moves = [
        pltpu.make_async_copy(src, dst, refs[-1].at[i])
        for i, (src, dst) in enumerate(zip(refs[:n], refs[n : 2 * n], strict=True))
    ]
    for move in moves:
        move.start()
    for move in moves:
        move.wait()


def fwd_kernel(q_ref, k_ref, v_ref, lw_ref, lo_ref, wq_ref):
    level = diag_level()
    rows, heads, _ = q_ref.shape
    q_all, k_all, v_all = flat(q_ref), flat(k_ref), flat(v_ref)
    for h in range(heads):
        lanes = slice(h * HD, (h + 1) * HD)
        q, k, v = q_all[:, lanes], k_all[:, lanes], v_all[:, lanes]
        for i in range(rows // BLK):
            n = (i + 1) * BLK
            st = dot(k[:n], q[i * BLK : n], NT)
            mix = mix_parts(lw_ref, level, h, i)
            at = jnp.concatenate(
                [(st[j * BLK : (j + 1) * BLK] * mix[j]).astype(BF16) for j in range(i + 1)],
                axis=0,
            )
            lo_ref[pl.ds(i * BLK, BLK), lanes] = dot(at, v[:n], TN)
        qt = q.astype(F32).T
        for j in range(FAR):
            row = lw_ref[NEAR + j, pl.ds(h, 1), :] * C[NEAR + j]
            wq_ref[h, pl.ds(j * HD, HD), :] = (qt * row).astype(BF16)


def bwd_kernel(first, q_ref, k_ref, v_ref, g_ref, lw_ref, dq_ref, dk_ref, dv_ref, ng_ref):
    level = diag_level()
    rows = q_ref.shape[0]
    blocks = rows // BLK
    q_all, k_all, v_all = flat(q_ref), flat(k_ref), flat(v_ref)
    for n_head in range(dq_ref.shape[1] // HD):
        h = first + n_head
        held = slice(h * HD, (h + 1) * HD)
        lanes = slice(n_head * HD, (n_head + 1) * HD)
        q, k, v, g = q_all[:, held], k_all[:, held], v_all[:, held], g_ref[:, held]
        for i in reversed(range(blocks)):
            n = (i + 1) * BLK
            q_i, g_i = q[i * BLK : n], g[i * BLK : n]
            st = dot(k[:n], q_i, NT)
            bt = dot(v[:n], g_i, NT)
            mix = mix_parts(lw_ref, level, h, i)
            ats, gts, sums = [], [], [None] * NEAR
            for j in range(i + 1):
                s_j = st[j * BLK : (j + 1) * BLK]
                b_j = bt[j * BLK : (j + 1) * BLK]
                ats.append((s_j * mix[j]).astype(BF16))
                gts.append((b_j * mix[j]).astype(BF16))
                prod = s_j * b_j
                if j == i:
                    for l in range(8):
                        sums[l] = jnp.sum(
                            jnp.where(level == l, prod, 0.0), axis=0, keepdims=True
                        )
                else:
                    l = 8 if (i ^ j) == 1 else 9
                    total = jnp.sum(prod, axis=0, keepdims=True)
                    sums[l] = total if sums[l] is None else sums[l] + total
            at = jnp.concatenate(ats, axis=0)
            gt = jnp.concatenate(gts, axis=0)
            for l in range(NEAR):
                value = jnp.zeros((1, BLK), F32) if sums[l] is None else sums[l] * C[l]
                ng_ref[n_head, pl.ds(l, 1), pl.ds(i * BLK, BLK)] = value
            dq_ref[pl.ds(i * BLK, BLK), lanes] = dot(gt, k[:n], TN)
            if i == blocks - 1:
                dk_ref[:, lanes] = dot(gt, q_i, NN)
                dv_ref[:, lanes] = dot(at, g_i, NN)
            else:
                dk_ref[pl.ds(0, n), lanes] += dot(gt, q_i, NN)
                dv_ref[pl.ds(0, n), lanes] += dot(at, g_i, NN)


def bit_of(axis, bit):
    return lax.rem(lax.div(lax.axis_index(axis), 1 << bit), 2)


def tree_bits():
    return [bit_of("y", 0), bit_of("y", 1), bit_of("z", 0), bit_of("z", 1), bit_of("z", 2)]


def left_stack(r_refs, h):
    return jnp.concatenate(
        [
            (r[h].astype(F32) * b.astype(F32)).astype(BF16)
            for b, r in zip(tree_bits(), r_refs, strict=True)
        ],
        axis=0,
    )


def attend_kernel(lo_ref, wq_ref, r0, r1, r2, r3, r4, att_ref):
    for h in range(wq_ref.shape[0]):
        lanes = slice(h * HD, (h + 1) * HD)
        states = left_stack((r0, r1, r2, r3, r4), h)
        att_ref[:, lanes] = (lo_ref[:, lanes] + dot(wq_ref[h], states, TN)).astype(BF16)


def dq_kernel(q_ref, g_ref, lw_ref, dqa, dqb, nga, ngb, r0, r1, r2, r3, r4, dq_ref, gl_ref):
    _, heads, _ = q_ref.shape
    q_all = flat(q_ref)
    outs = []
    for h in range(heads):
        lanes = slice(h * HD, (h + 1) * HD)
        states = left_stack((r0, r1, r2, r3, r4), h)
        read = dot(states, g_ref[:, lanes], NT)
        qt = q_all[:, lanes].astype(F32).T
        total = jnp.zeros(qt.shape, F32)
        for j in range(FAR):
            part = read[j * HD : (j + 1) * HD]
            row = lw_ref[NEAR + j, pl.ds(h, 1), :] * C[NEAR + j]
            total = total + part * row
            gl_ref[NEAR + j, pl.ds(h, 1), :] = (
                jnp.sum(part * qt, axis=0, keepdims=True) * C[NEAR + j]
            )
        local, near, at = (dqa, nga, h) if h < heads // 2 else (dqb, ngb, h - heads // 2)
        for l in range(NEAR):
            gl_ref[l, pl.ds(h, 1), :] = near[at, pl.ds(l, 1), :]
        outs.append((local[:, at * HD : (at + 1) * HD] + total.T).astype(BF16))
    dq_ref[...] = jnp.concatenate(outs, axis=1).reshape(q_ref.shape)


def swapped(m):
    b0, b1 = bit_of("y", 0), bit_of("y", 1)
    low = 1 - b0 if m & 1 else b0
    high = 1 - b1 if m & 2 else b1
    return high * 2 + low


def state_kernel(own_ref, rec_ref, wq_ref, g_ref, *ws_refs):
    g_ref[...] = (own_ref[...] + rec_ref[...].astype(F32)).astype(BF16)
    for m, ws_ref in enumerate(ws_refs):
        h = swapped(m)
        g = g_ref[:, pl.ds(pl.multiple_of(h * HD, HD), HD)]
        ws_ref[...] = dot(wq_ref[h], g, NN).astype(BF16).reshape(FAR, HD, HD)


def rsum_kernel(w0, w1, w2, w3, near_ref, held_ref, send_ref):
    w = (w0, w1, w2, w3)
    b0, b1 = bit_of("y", 0), bit_of("y", 1)
    low = [(1 - b0 if n & 1 else b0).astype(F32) for n in range(4)]
    high = [(1 - b1 if n & 2 else b1).astype(F32) for n in range(4)]
    first = [w[n][0].astype(F32) * low[n] for n in range(4)]
    second = [w[n][1].astype(F32) * high[n] for n in range(4)]
    for m in range(4):
        near_ref[m] = first[m ^ 1] + second[m ^ 2] + second[m ^ 3]
    for j in range(2, FAR):
        total = sum(w[n][j].astype(F32) for n in range(4))
        held_ref[j - 2] = total
        send_ref[j - 2] = total.astype(BF16)


def tree0_kernel(held_ref, got_ref, acc_ref, next_ref, send_ref):
    off = (1 - bit_of("z", 0)).astype(F32)
    acc_ref[...] = got_ref[0].astype(F32) * off
    for j in range(2):
        total = held_ref[j + 1] + got_ref[j + 1].astype(F32)
        next_ref[j] = total
        send_ref[j] = total.astype(BF16)


def tree1_kernel(acc_in, held_ref, got_ref, acc_ref, send_ref):
    off = (1 - bit_of("z", 1)).astype(F32)
    acc_ref[...] = acc_in[...] + got_ref[0].astype(F32) * off
    send_ref[0] = (held_ref[1] + got_ref[1].astype(F32)).astype(BF16)


def tree2_kernel(acc_in, near_ref, got_ref, *out_refs):
    off = (1 - bit_of("z", 2)).astype(F32)
    acc = acc_in[...] + got_ref[0].astype(F32) * off
    for m, ref in enumerate(out_refs):
        ref[...] = (near_ref[m] + acc).astype(BF16)


def final_kernel(dka, dva, dkb, dvb, k_ref, v_ref, r0, r1, r2, r3, dk_ref, dv_ref, r_ref):
    k_all, v_all = flat(k_ref), flat(v_ref)
    for m, r in enumerate((r0, r1, r2, r3)):
        r_ref[swapped(m)] = r[...]
    dks, dvs = [], []
    for h in range(r_ref.shape[0]):
        lanes = slice(h * HD, (h + 1) * HD)
        r = r_ref[h]
        half = r_ref.shape[0] // 2
        dkl, dvl, at = (dka, dva, h) if h < half else (dkb, dvb, h - half)
        part = slice(at * HD, (at + 1) * HD)
        dks.append((dkl[:, part] + dot(v_all[:, lanes], r, NT)).astype(BF16))
        dvs.append((dvl[:, part] + dot(k_all[:, lanes], r, NN)).astype(BF16))
    dk_ref[...] = jnp.concatenate(dks, axis=1).reshape(k_ref.shape)
    dv_ref[...] = jnp.concatenate(dvs, axis=1).reshape(k_ref.shape)


def wcol(ref, n, seg):
    steps = (0, NX - 1, 1, 2)[n]
    at = lax.rem(lax.axis_index("x") + steps, NX) * 2 + lax.axis_index("c")
    return ref[:, pl.ds(pl.multiple_of(at * seg, seg), seg)]


def mix12_kernel(go, gl, gr, w_ref, p_ref, own_ref, par_ref):
    seg = go.shape[1]
    for ref, out in ((p_ref, par_ref), (w_ref, own_ref)):
        out[...] = (
            dot(go[...], wcol(ref, 0, seg), NT)
            + dot(gl[...], wcol(ref, 1, seg), NT)
            + dot(gr[...], wcol(ref, 2, seg), NT)
        )


def mix3_kernel(top, bot, acc, w_ref, out_ref):
    half, seg = top.shape
    w = wcol(w_ref, 3, seg)
    for base, part in ((0, top), (half, bot)):
        rows = pl.ds(base, half)
        out_ref[rows, :] = (acc[rows, :] + dot(part[...], w, NT)).astype(out_ref.dtype)


def out_rows(a, ap, w_ref, p_ref, n, rows, seg):
    return dot(a[rows, :], wcol(w_ref, n, seg), NN) + dot(
        ap[rows, :], wcol(p_ref, n, seg), NN
    )


def out_far_kernel(a, ap, w_ref, p_ref, top_ref, bot_ref):
    half, seg = top_ref.shape
    for ref, base in ((top_ref, 0), (bot_ref, half)):
        ref[...] = out_rows(a, ap, w_ref, p_ref, 3, pl.ds(base, half), seg).astype(BF16)


def out_rest_kernel(a, ap, w_ref, p_ref, r_bot, l_top, r_top, l_bot, own):
    half, seg = r_bot.shape
    top, bot = pl.ds(0, half), pl.ds(half, half)
    r_bot[...] = out_rows(a, ap, w_ref, p_ref, 2, bot, seg).astype(BF16)
    l_top[...] = out_rows(a, ap, w_ref, p_ref, 1, top, seg).astype(BF16)
    r_top[...] = out_rows(a, ap, w_ref, p_ref, 2, top, seg)
    l_bot[...] = out_rows(a, ap, w_ref, p_ref, 1, bot, seg)
    own[...] = out_rows(a, ap, w_ref, p_ref, 0, pl.ds(0, 2 * half), seg)


def join_kernel(r_top, l_bot, via_l, via_r, r_out, l_out):
    r_out[...] = (r_top[...] + via_l[...].astype(F32)).astype(BF16)
    l_out[...] = (l_bot[...] + via_r[...].astype(F32)).astype(BF16)


def sum_kernel(own, l_top, l_bot, r_top, r_bot, out_ref):
    half = l_top.shape[0]
    for base, a, b in ((0, l_top, r_top), (half, l_bot, r_bot)):
        rows = pl.ds(base, half)
        out_ref[rows, :] = (own[rows, :] + a[...].astype(F32) + b[...].astype(F32)).astype(BF16)


VMEM = pl.BlockSpec(memory_space=pltpu.VMEM)
HBM = pl.BlockSpec(memory_space=pltpu.HBM)


def kernel_call(body, outs, operands, flops, scratch=(), space=VMEM, vmem=16):
    out_shape = [jax.ShapeDtypeStruct(s, d) for s, d in outs]
    nbytes = sum(math.prod(s) * jnp.dtype(d).itemsize for s, d in outs)
    nbytes += sum(o.size * o.dtype.itemsize for o in operands)
    return pl.pallas_call(
        body,
        in_specs=[space] * len(operands),
        out_specs=[VMEM] * len(outs),
        out_shape=out_shape,
        scratch_shapes=list(scratch),
        cost_estimate=pl.CostEstimate(
            flops=int(flops), transcendentals=0, bytes_accessed=int(nbytes)
        ),
        compiler_params=pltpu.CompilerParams(vmem_limit_bytes=vmem << 20),
    )(*operands)


def body(queries, key_matrix, value_matrix, level_weight, out_weight, grad_out):
    rows, heads, hd = queries.shape
    width = heads * hd
    feat = out_weight.shape[2]
    levels = level_weight.shape[0]
    half = rows // 2
    nx, ny, nz = (lax.axis_size(n) for n in ("x", "y", "z"))
    right = [(i, (i + 1) % nx) for i in range(nx)]
    left = [(i, (i - 1) % nx) for i in range(nx)]
    swap = [(0, 1), (1, 0)]
    seg = feat // (2 * nx)
    w2 = out_weight.reshape(width, feat)

    from_l = lax.ppermute(grad_out, "x", right)
    from_r = lax.ppermute(grad_out, "x", left)
    w_par = lax.ppermute(w2, "c", swap)

    run = jnp.einsum("gpl,gpq->plq", key_matrix, value_matrix, preferred_element_type=F32)
    inputs = [
        pltpu.with_memory_space_constraint(i, pltpu.HBM)
        for i in (queries, key_matrix, value_matrix, level_weight)
    ]
    queries, key_matrix, value_matrix, level_weight = kernel_call(
        stage_kernel,
        [(i.shape, i.dtype) for i in inputs],
        inputs,
        0,
        scratch=[pltpu.SemaphoreType.DMA((4,))],
        space=HBM,
    )
    lefts = []
    for axis, mask in (("y", 1), ("y", 3), ("z", 1), ("z", 2), ("z", 6)):
        route = [(i, i ^ mask) for i in range(lax.axis_size(axis))]
        got = lax.ppermute(run.astype(BF16), axis, route)
        lefts.append(got)
        run = run + got.astype(F32)
    block = 2 * rows * rows * width
    local_out, wq = kernel_call(
        fwd_kernel,
        [((rows, width), F32), ((heads, FAR * hd, rows), BF16)],
        (queries, key_matrix, value_matrix, level_weight),
        2 * block,
    )

    far_top = lax.ppermute(from_l[:half], "x", right)
    far_bot = lax.ppermute(from_r[half:], "x", left)
    mm = 2 * rows * seg * width
    own12, par12 = kernel_call(
        mix12_kernel, [((rows, width), F32)] * 2, (grad_out, from_l, from_r, w2, w_par), 6 * mm
    )
    (mix_send,) = kernel_call(
        mix3_kernel, [((rows, width), BF16)], (far_top, far_bot, par12, w_par), mm
    )
    mix_got = lax.ppermute(mix_send, "c", swap)
    (mix_own,) = kernel_call(mix3_kernel, [((rows, width), F32)], (far_top, far_bot, own12, w2), mm)
    square = (hd, hd)
    g2, *ws = kernel_call(
        state_kernel,
        [((rows, width), BF16)] + [((FAR, *square), BF16)] * ny,
        (mix_own, mix_got, wq),
        2 * rows * hd * hd * FAR * heads,
    )

    def across_y(parts):
        arrived = [parts[0]]
        for m in range(1, ny):
            arrived.append(lax.ppermute(parts[m], "y", [(i, i ^ m) for i in range(ny)]))
        return arrived

    def across_z(bit, value):
        return lax.ppermute(value, "z", [(i, i ^ (1, 2, 6)[bit]) for i in range(nz)])

    tiny = 8 * hd * hd
    near, held, send = kernel_call(
        rsum_kernel,
        [((ny, *square), F32), ((3, *square), F32), ((3, *square), BF16)],
        across_y(ws),
        tiny,
    )
    acc, held, send = kernel_call(
        tree0_kernel,
        [(square, F32), ((2, *square), F32), ((2, *square), BF16)],
        (held, across_z(0, send)),
        tiny,
    )
    acc, send = kernel_call(
        tree1_kernel, [(square, F32), ((1, *square), BF16)], (acc, held, across_z(1, send)), tiny
    )
    back = kernel_call(tree2_kernel, [(square, BF16)] * ny, (acc, near, across_z(2, send)), tiny)
    right_states = across_y(back)

    (attended,) = kernel_call(
        attend_kernel,
        [((rows, width), BF16)],
        (local_out, wq, *lefts),
        2 * rows * hd * hd * FAR * heads,
    )
    att_par = lax.ppermute(attended, "c", swap)

    piece = ((half, seg), BF16)
    piece32 = ((half, seg), F32)
    operands = (attended, att_par, w2, w_par)
    opp_top, opp_bot = kernel_call(out_far_kernel, [piece] * 2, operands, 2 * mm)
    via_l = lax.ppermute(opp_top, "x", right)
    via_r = lax.ppermute(opp_bot, "x", left)
    r_bot, l_top, r_top, l_bot, out_own = kernel_call(
        out_rest_kernel, [piece] * 2 + [piece32] * 2 + [((rows, seg), F32)], operands, 6 * mm
    )
    in_l_bot = lax.ppermute(r_bot, "x", right)
    in_r_top = lax.ppermute(l_top, "x", left)
    r_top, l_bot = kernel_call(
        join_kernel, [piece] * 2, (r_top, l_bot, via_l, via_r), rows * seg * 2
    )
    in_l_top = lax.ppermute(r_top, "x", right)
    in_r_bot = lax.ppermute(l_bot, "x", left)
    (mixed_out,) = kernel_call(
        sum_kernel,
        [((rows, seg), BF16)],
        (out_own, in_l_top, in_l_bot, in_r_top, in_r_bot),
        rows * seg * 4,
    )

    def backward(first):
        two = heads // 2
        return kernel_call(
            functools.partial(bwd_kernel, first),
            [((rows, two * hd), F32)] * 3 + [((two, NEAR, rows), F32)],
            (queries, key_matrix, value_matrix, g2, level_weight),
            2.5 * block,
        )

    dq_a, dk_a, dv_a, near_a = backward(0)
    dq_b, dk_b, dv_b, near_b = backward(heads // 2)
    grad_queries, grad_levels = kernel_call(
        dq_kernel,
        [((rows, heads, hd), BF16), ((levels, heads, rows), F32)],
        (queries, g2, level_weight, dq_a, dq_b, near_a, near_b, *lefts),
        2 * rows * hd * hd * FAR * heads,
    )
    grad_keys, grad_values = kernel_call(
        final_kernel,
        [((rows, heads, hd), BF16)] * 2,
        (dk_a, dv_a, dk_b, dv_b, key_matrix, value_matrix, *right_states),
        4 * rows * hd * hd * heads,
        scratch=[pltpu.VMEM((heads, hd, hd), BF16)],
    )
    return mixed_out, grad_queries, grad_keys, grad_values, grad_levels


def solution(mesh):
    grid = Mesh(mesh.devices.reshape(8, 4, 4, 2), ("z", "y", "x", "c"))
    seq, head = ("z", "y"), ("x", "c")
    by_row = P(seq, head, None)
    in_specs = (by_row, by_row, by_row, P(None, head, seq), P(head, None, None), P(seq, head))
    out_specs = (P(seq, head), by_row, by_row, by_row, P(None, head, seq))
    return jax.shard_map(body, mesh=grid, in_specs=in_specs, out_specs=out_specs, check_vma=False)
```
